32 devices in a mesh: row: 4 (over x, core), col: 8 (over z, y).
Axes of the slice: x: 2, y: 2, z: 4, core: 2. Of those that a mesh axis runs over, the one named last changes fastest.
Arguments:
- eigvecs: float32 [1024, 1024], P('row', 'col'), may hold values from -6 to 6
- offsets: int32 [1], replicated, may hold values from 0 to 127
- plan: int32 [1, 6], replicated, may hold values from 0 to 7
- refl_v: float32 [8, 255, 128], P('col')
- refl_t: float32 [8, 128, 128], P('col'), as said below
Outputs:
- updated: float32 [1024, 1024], P('row', 'col')
The draws below stay inside these ranges and needn't reach their ends.
Inputs may be any that keep to these rules, and one draw needn't show every extreme that they name: For each bank entry, I - refl_v refl_t refl_v^T is orthogonal up to rounding.
All inputs are finite; a program needn't handle non-finite values.
Results may differ from the reference program's by a relative error of at most 0.00015.
Values sent between devices are 32-bit elements; how exact they have to be, the bound alone decides.
No kernel may reach another device: no remote copies, remote signals or barrier semaphores. Data moves between devices by JAX's collectives and lax.ppermute only.
A program may use at most 64 MiB of HBM per device.

```python
import jax
import jax.numpy as jnp
from jax import lax

NB = 128
SWEEPS = 1
ROWS = 1024
COLS = 1024
BANK = 8
BLOCKS = 6


HIGHEST = lax.Precision.HIGHEST


def build_factor(vectors):
    gram_matrix = jnp.dot(vectors.T, vectors, precision=HIGHEST)
    positions = jnp.arange(NB)

    def add_column(column, factor):
        house_scale = 2.0 / gram_matrix[column, column]
        correlation = jnp.where(positions < column, gram_matrix[:, column], 0.0)
        entries = -house_scale * jnp.dot(factor, correlation, precision=HIGHEST)
        entries = entries + house_scale * (positions == column).astype(jnp.float32)
        return factor.at[:, column].set(entries)
    return lax.fori_loop(0, NB, add_column, jnp.zeros((NB, NB), jnp.float32))


def make_bank(key):
    subkey = jax.random.fold_in(key, 7)
    row_ids = jnp.arange(2 * NB - 1)[:, None]
    col_ids = jnp.arange(NB)[None, :]
    inside = (row_ids > col_ids) & (row_ids < col_ids + NB)
    entries = 0.1 * jax.random.normal(subkey, (BANK, 2 * NB - 1, NB), jnp.float32)
    vectors = jnp.where(inside[None], entries, 0.0) + (row_ids == col_ids).astype(jnp.float32)[None]
    factors = lax.map(build_factor, vectors)
    return (vectors, factors)


def draw_refl_v(key, part):
    return make_bank(key)[0]


def draw_refl_t(key, part):
    return make_bank(key)[1]


def touch_ends(values, own_key, least, top_value):
    longest = values.shape.index(max(values.shape))
    spots = []
    for shift in (0, 1):
        where = [jax.random.randint(jax.random.fold_in(own_key, axis), (), 0, length) for axis, length in enumerate(values.shape)]
        where[longest] = (where[longest] + shift) % values.shape[longest]
        spots.append(tuple(where))
    return values.at[spots[0]].set(least).at[spots[1]].set(top_value)


def block_scale(rng, extent, shards, low, top_value):
    def one(axis_at, shards_of):
        steps = jax.random.uniform(jax.random.fold_in(jax.random.fold_in(rng, 6), axis_at), (shards_of,), jnp.float32, low / len(shards), top_value / len(shards))
        return jnp.repeat(jnp.exp(steps), extent[axis_at] // shards_of).reshape((-1,) + (1,) * (len(extent) - axis_at - 1))

    gain = one(*shards[0])
    for cut in shards[1:]:
        gain = gain * one(*cut)
    return gain


def scatter_about(key, dims, width, most, shards=(), dtype=jnp.bfloat16):
    factor_of = block_scale(key, dims, shards, -0.22, 0.18) if shards else 1.0
    values = jax.random.normal(key, dims, jnp.float32) * width * factor_of
    return jnp.minimum(jnp.maximum(values, -most), most).astype(dtype)


def setup_inputs(seed: int = 0) -> dict:
    key_list = jax.random.split(jax.random.key(seed), 6)
    eigvecs = scatter_about(key_list[0], (ROWS, COLS), 1.0, 6.0, ((0, 4), (1, 8)), jnp.float32)
    offsets = jax.random.randint(key_list[1], (SWEEPS,), 0, NB).astype(jnp.int32)
    plan = touch_ends(jax.random.randint(key_list[2], (SWEEPS, BLOCKS), 0, BANK), jax.random.fold_in(key_list[2], 1), 0, BANK - 1).astype(jnp.int32)
    refl_v = draw_refl_v(jax.random.fold_in(key_list[5], 71), 0)
    refl_t = draw_refl_t(jax.random.fold_in(key_list[5], 71), 0)
    return {"eigvecs": eigvecs, "offsets": offsets, "plan": plan, "refl_v": refl_v, "refl_t": refl_t}


HIGHEST = lax.Precision.HIGHEST


def reference(eigvecs, offsets, plan, refl_v, refl_t):
    matrix = eigvecs
    for sweep in range(SWEEPS):
        first_row = offsets[sweep].astype(jnp.int32)

        def apply_block(index, matrix):
            index = jnp.asarray(index).astype(jnp.int32)
            row_start = (first_row + index * NB).astype(jnp.int32)
            block_rows = lax.dynamic_slice_in_dim(matrix, row_start, 2 * NB - 1, 0)
            block_id = plan[sweep, index]
            vectors = refl_v[block_id]
            factor = refl_t[block_id]
            inner_prod = jnp.dot(vectors.T, block_rows, precision=HIGHEST)
            scaled = jnp.dot(factor, inner_prod, precision=HIGHEST)
            block_rows = block_rows - jnp.dot(vectors, scaled, precision=HIGHEST)
            return lax.dynamic_update_slice_in_dim(matrix, block_rows, row_start, 0)

        matrix = lax.fori_loop(0, BLOCKS, apply_block, matrix)
    return matrix
```

```python
import functools

import jax
import jax.numpy as jnp
from jax import lax
from jax.experimental import pallas as pl
from jax.experimental.pallas import tpu as pltpu
from jax.sharding import PartitionSpec as P

AXES = ("row", "col")
F32, BF16 = jnp.float32, jnp.bfloat16
NT = (((1,), (1,)), ((), ()))


def iotas(rows, cols):
    return lax.broadcasted_iota(jnp.int32, (rows, cols), 0), lax.broadcasted_iota(jnp.int32, (rows, cols), 1)


def pack_kernel(v_ref, t_ref, wire_ref):
    nb = t_ref.shape[0]
    half = nb // 2
    row, col = iotas(nb, nb)
    low = v_ref[0:nb, :]
    up = pltpu.roll(v_ref[nb - 1 : 2 * nb - 1, :], nb - 1, axis=0)
    factor = t_ref[...]
    wire_ref[0:nb, :] = jnp.where(row > col, low, jnp.where(row < col, up, factor))
    turned = jnp.transpose(jnp.concatenate([factor[half:, :], factor[:half, :]], axis=0))[half:, :]
    row, col = iotas(half, nb)
    wire_ref[nb:, :] = jnp.where(row < col, factor[:half, :], turned)


def pack(vectors, factor):
    nb = factor.shape[0]
    return pl.pallas_call(
        pack_kernel,
        out_shape=jax.ShapeDtypeStruct((nb + nb // 2, nb), F32),
        name="pack",
    )(vectors, factor)


def split(x):
    high = x.astype(BF16)
    return high, (x - high.astype(F32)).astype(BF16)


def dot(a, b, dims=(((1,), (0,)), ((), ()))):
    return lax.dot_general(a, b, dims, preferred_element_type=F32)


def dot3(a, b, dims=(((1,), (0,)), ((), ()))):
    return dot(a[0], b[0], dims) + (dot(a[1], b[0], dims) + dot(a[0], b[1], dims))


def apply_kernel(
    n_col, n_row, n_blocks, off_ref, plan_ref, *refs
):
    banks, refs = refs[:n_col], refs[n_col:]
    parts, refs = refs[:n_row], refs[n_row:]
    out_ref, rows_ref, low_ref, up_ref, lead_ref, solved_ref = refs
    nb = banks[0].shape[1]
    half = nb // 2
    own_rows = parts[0].shape[0]
    my_row, my_col = lax.axis_index("row"), lax.axis_index("col")
    odd = lax.rem(my_row, 2)
    first = off_ref[0]

    for step in range(n_row):
        start = pl.multiple_of(jnp.bitwise_xor(my_row, step) * own_rows + nb, nb)
        rows_ref[pl.ds(start, own_rows), :] = parts[step][...]

    row, col = iotas(nb, nb)
    lower, upper, diagonal = row > col, row < col, row == col
    row_h, col_h = iotas(half, nb)
    for slot in range(n_col):
        distance = slot_distance(slot, n_col, odd)
        entry = jnp.bitwise_xor(my_col, distance)
        packed = banks[slot][0:nb, :]
        tail = banks[slot][nb:, :]
        low = split(jnp.where(lower, packed, diagonal.astype(F32)))
        up = split(jnp.where(upper, packed, 0.0))
        below = jnp.where(row_h > col_h, tail, 0.0)
        turned = jnp.transpose(jnp.concatenate([jnp.zeros_like(below), below], axis=0))[:half, :]
        factor = jnp.concatenate([jnp.where(row_h < col_h, tail, 0.0), turned], axis=0)
        factor = split(jnp.where(diagonal, packed, factor))
        lead = [dot3(factor, low, NT), dot3(factor, up, NT)]
        lead = split(jnp.concatenate(lead, axis=1))
        for i in range(2):
            low_ref[entry, i] = low[i]
            up_ref[entry, i] = up[i]
            lead_ref[entry, i] = lead[i]

    zero = jnp.zeros((nb, out_ref.shape[1]), BF16)
    for i in range(2):
        solved_ref[0, i] = zero
        solved_ref[1, i] = zero
        solved_ref[n_blocks + 2, i] = zero
        solved_ref[n_blocks + 3, i] = zero

    def block(index):
        entry = plan_ref[0, index]
        before = plan_ref[0, jnp.maximum(index - 1, 0)]
        window = split(rows_ref[pl.ds(first + (index + 1) * nb, 2 * nb), :])
        lead = lead_ref[entry, 0], lead_ref[entry, 1]
        free = dot3(lead, window)
        link = split(dot3([x[:, :nb] for x in lead], (up_ref[before, 0], up_ref[before, 1])))
        return free, link

    def store(index, value):
        value = split(value)
        for i in range(2):
            solved_ref[index + 2, i] = value[i]
        return value

    if n_blocks <= 8:
        work = [block(index) for index in range(n_blocks)]
        last = store(0, work[0][0])
        for index in range(1, n_blocks):
            free, link = work[index]
            last = store(index, free - dot3(link, last))
    else:
        store(0, block(0)[0])

        def step(index, carry):
            free, link = block(index)
            store(index, free - dot3(link, (solved_ref[index + 1, 0], solved_ref[index + 1, 1])))
            return carry

        lax.fori_loop(1, n_blocks, step, 0)

    mine = my_row * own_rows
    tile = lax.div(mine - first + nb, nb) - 1
    n_tiles = own_rows // nb + 1
    for k in range(n_tiles):
        t = jnp.minimum(tile + k, n_blocks + 1)
        low_entry = plan_ref[0, jnp.clip(t, 0, n_blocks - 1)]
        up_entry = plan_ref[0, jnp.clip(t - 1, 0, n_blocks - 1)]
        start = first + (t + 1) * nb
        value = rows_ref[pl.ds(start, nb), :]
        value = value - (
            dot3((up_ref[up_entry, 0], up_ref[up_entry, 1]), (solved_ref[t + 1, 0], solved_ref[t + 1, 1]))
            + dot3((low_ref[low_entry, 0], low_ref[low_entry, 1]), (solved_ref[t + 2, 0], solved_ref[t + 2, 1]))
        )
        rows_ref[pl.ds(start, nb), :] = value
    out_ref[...] = rows_ref[pl.ds(pl.multiple_of(mine + nb, nb), own_rows), :]


def slot_distance(slot, n_col, odd):
    pairs = n_col // 2
    if slot == 0:
        return jnp.int32(0)
    step = (slot - 1) % pairs
    even_distance, odd_distance = n_col - 1 - 2 * step, n_col - 2 - 2 * step
    if step == pairs - 1:
        return jnp.int32(1)
    if slot > pairs:
        even_distance, odd_distance = odd_distance, even_distance
    return even_distance + odd * (odd_distance - even_distance)


def on_device(eigvecs, offsets, plan, refl_v, refl_t):
    n_row, n_col = lax.axis_size("row"), lax.axis_size("col")
    own_rows, own_cols = eigvecs.shape
    nb = refl_t.shape[2]
    n_blocks = plan.shape[1]
    pairs = n_col // 2

    def send(x, row_by, col_by):
        to = [
            (r * n_col + c, (r ^ row_by) * n_col + (c ^ col_by[r % 2]))
            for r in range(n_row)
            for c in range(n_col)
        ]
        return lax.ppermute(x, AXES, to)

    wire = pack(refl_v.reshape(refl_v.shape[1:]), refl_t.reshape(refl_t.shape[1:]))
    got = []
    for step in range(pairs):
        by = (n_col - 1 - 2 * step, n_col - 2 - 2 * step)
        if step == pairs - 1:
            by = (1, 1)
        got.append(send(wire, 0, by))
    parts = {0: eigvecs}
    for step in range(2, n_row, 2):
        parts[step] = send(eigvecs, step, (0, 0))
    banks = [wire] + got + [send(x, 1, (0, 0)) for x in got[:-1]]
    for step in range(0, n_row, 2):
        parts[step + 1] = send(parts[step], 1, (0, 0))
    parts = [parts[step] for step in range(n_row)]

    vmem = pl.BlockSpec(memory_space=pltpu.VMEM)
    smem = pl.BlockSpec(memory_space=pltpu.SMEM)
    return pl.pallas_call(
        functools.partial(apply_kernel, n_col, n_row, n_blocks),
        out_shape=jax.ShapeDtypeStruct((own_rows, own_cols), F32),
        in_specs=[smem, smem] + [vmem] * (n_col + n_row),
        out_specs=vmem,
        scratch_shapes=[
            pltpu.VMEM((n_row * own_rows + 3 * nb, own_cols), F32),
            pltpu.VMEM((n_col, 2, nb, nb), BF16),
            pltpu.VMEM((n_col, 2, nb, nb), BF16),
            pltpu.VMEM((n_col, 2, nb, 2 * nb), BF16),
            pltpu.VMEM((n_blocks + 4, 2, nb, own_cols), BF16),
        ],
        name="apply_blocks",
    )(offsets, plan, *banks, *parts)


def solution(mesh):
    in_specs = (P("row", "col"), P(), P(), P("col", None, None), P("col", None, None))
    return jax.shard_map(
        on_device, mesh=mesh, in_specs=in_specs, out_specs=P("row", "col"), check_vma=False
    )
```

```python
import functools

import jax
import jax.numpy as jnp
from jax import lax
from jax.experimental import pallas as pl
from jax.experimental.pallas import tpu as pltpu
from jax.sharding import PartitionSpec as P


AXES = ("row", "col")
F32, BF16 = jnp.float32, jnp.bfloat16
NT = (((1,), (1,)), ((), ()))


def iotas(rows, cols):
    return lax.broadcasted_iota(jnp.int32, (rows, cols), 0), lax.broadcasted_iota(jnp.int32, (rows, cols), 1)


def pack_kernel(both_any, wire_ref, both_ref, sem):
    nb = wire_ref.shape[1]
    half = nb // 2
    copy = pltpu.make_async_copy(both_any.at[:, 0, :], both_ref.at[0 : 3 * nb - 1], sem)
    copy.start()
    copy.wait()
    row, col = iotas(nb, nb)
    factor = both_ref[0:nb, :]
    low = both_ref[nb : 2 * nb, :]
    up = pltpu.roll(both_ref[2 * nb - 1 : 3 * nb - 1, :], nb - 1, axis=0)
    wire_ref[0:nb, :] = jnp.where(row > col, low, jnp.where(row < col, up, factor))
    turned = jnp.transpose(jnp.concatenate([factor[half:, :], factor[:half, :]], axis=0))[half:, :]
    row, col = iotas(half, nb)
    wire_ref[nb:, :] = jnp.where(row < col, factor[:half, :], turned)


def pack(vectors, factor):
    nb = factor.shape[2]
    both = jnp.concatenate([factor.reshape(nb, 1, nb), jnp.transpose(vectors, (1, 0, 2))], axis=0)
    return pl.pallas_call(
        pack_kernel,
        out_shape=jax.ShapeDtypeStruct((nb + nb // 2, nb), F32),
        in_specs=[pl.BlockSpec(memory_space=pl.ANY)],
        out_specs=pl.BlockSpec(memory_space=pltpu.VMEM),
        scratch_shapes=[pltpu.VMEM((3 * nb, nb), F32), pltpu.SemaphoreType.DMA],
        compiler_params=pltpu.CompilerParams(vmem_limit_bytes=4 * 2**20),
        name="pack",
    )(both)


def split(x):
    high = x.astype(BF16)
    return high, (x - high.astype(F32)).astype(BF16)


def dot(a, b, dims=(((1,), (0,)), ((), ()))):
    return lax.dot_general(a, b, dims, preferred_element_type=F32)


def dot3(a, b, dims=(((1,), (0,)), ((), ()))):
    return dot(a[0], b[0], dims) + (dot(a[1], b[0], dims) + dot(a[0], b[1], dims))


def unpack(packed):
    nb = packed.shape[1]
    half = nb // 2
    row, col = iotas(nb, nb)
    row_h, col_h = iotas(half, nb)
    diagonal = row == col
    square, tail = packed[:nb], packed[nb:]
    low = split(jnp.where(row > col, square, diagonal.astype(F32)))
    up = split(jnp.where(row < col, square, 0.0))
    below = jnp.where(row_h > col_h, tail, 0.0)
    turned = jnp.transpose(jnp.concatenate([jnp.zeros_like(below), below], axis=0))[:half, :]
    factor = jnp.concatenate([jnp.where(row_h < col_h, tail, 0.0), turned], axis=0)
    factor = split(jnp.where(diagonal, square, factor))
    return low + up + split(dot3(factor, low, NT)) + split(dot3(factor, up, NT))


def unpack_into(pieces_ref, banks, slots, n_col):
    odd = lax.rem(lax.axis_index("row"), 2)
    my_col = lax.axis_index("col")
    for bank, slot in zip(banks, slots):
        entry = jnp.bitwise_xor(my_col, slot_distance(slot, n_col, odd))
        for i, piece in enumerate(unpack(bank[...])):
            pieces_ref[entry, i] = piece


def near_kernel(n_col, slots, *refs):
    unpack_into(refs[-1], refs[:-1], slots, n_col)


def apply_kernel(n_col, n_row, n_blocks, slots, *refs):
    table_any, refs = refs[0], refs[1:]
    banks, refs = refs[: len(slots)], refs[len(slots) :]
    parts, refs = refs[:n_row], refs[n_row:]
    _, out_any, pieces_ref, rows_ref, solved_ref, plan_ref, sems = refs
    nb = banks[0].shape[1]
    own_rows, own_cols = parts[0].shape
    my_row = lax.axis_index("row")
    table = pltpu.make_async_copy(table_any, plan_ref, sems.at[0])
    table.start()

    for step in range(n_row):
        start = pl.multiple_of(jnp.bitwise_xor(my_row, step) * own_rows + nb, nb)
        rows_ref[pl.ds(start, own_rows), :] = parts[step][...]
    unpack_into(pieces_ref, banks, slots, n_col)

    zero = jnp.zeros((nb, own_cols), BF16)
    for index in (0, 1, n_blocks + 2, n_blocks + 3):
        for i in range(2):
            solved_ref[index, i] = zero
    table.wait()
    first = plan_ref[0, n_blocks]

    def low_of(entry):
        return pieces_ref[entry, 0], pieces_ref[entry, 1]

    def up_of(entry):
        return pieces_ref[entry, 2], pieces_ref[entry, 3]

    def block(index):
        entry = plan_ref[0, index]
        before = plan_ref[0, jnp.maximum(index - 1, 0)]
        window = split(rows_ref[pl.ds(first + (index + 1) * nb, 2 * nb), :])
        lead_low = pieces_ref[entry, 4], pieces_ref[entry, 5]
        lead = [jnp.concatenate([lead_low[i], pieces_ref[entry, 6 + i]], axis=1) for i in range(2)]
        free = dot3(lead, window)
        link = split(dot3(lead_low, up_of(before)))
        return free, link

    def store(index, value):
        value = split(value)
        for i in range(2):
            solved_ref[index + 2, i] = value[i]
        return value

    def solved_of(index):
        return solved_ref[index + 2, 0], solved_ref[index + 2, 1]

    if n_blocks <= 8:
        work = [block(index) for index in range(n_blocks)]
        last = store(0, work[0][0])
        for index in range(1, n_blocks):
            free, link = work[index]
            last = store(index, free - dot3(link, last))
    else:
        store(0, block(0)[0])

        def step(index, carry):
            free, link = block(index)
            store(index, free - dot3(link, solved_of(index - 1)))
            return carry

        lax.fori_loop(1, n_blocks, step, 0)

    mine = my_row * own_rows
    tile = lax.div(mine - first + nb, nb) - 1
    copies = []
    for k in range(own_rows // nb + 1):
        t = jnp.minimum(tile + k, n_blocks + 1)
        low_entry = plan_ref[0, jnp.clip(t, 0, n_blocks - 1)]
        up_entry = plan_ref[0, jnp.clip(t - 1, 0, n_blocks - 1)]
        window = pl.ds(first + (t + 1) * nb, nb)
        moved = dot3(up_of(up_entry), solved_of(t - 1)) + dot3(low_of(low_entry), solved_of(t))
        rows_ref[window, :] = rows_ref[window, :] - moved
        if k > 0:
            source = pl.ds(pl.multiple_of(mine + k * nb, nb), nb)
            copy = pltpu.make_async_copy(
                rows_ref.at[source, :], out_any.at[pl.ds((k - 1) * nb, nb), :], sems.at[k]
            )
            copy.start()
            copies.append(copy)
    for copy in copies:
        copy.wait()


def slot_distance(slot, n_col, odd):
    pairs = n_col // 2
    if slot == 0:
        return jnp.int32(0)
    step = (slot - 1) % pairs
    even_distance, odd_distance = n_col - 1 - 2 * step, n_col - 2 - 2 * step
    if step == pairs - 1:
        return jnp.int32(1)
    if slot > pairs:
        even_distance, odd_distance = odd_distance, even_distance
    return even_distance + odd * (odd_distance - even_distance)


def on_device(eigvecs, offsets, plan, refl_v, refl_t):
    n_row, n_col = lax.axis_size("row"), lax.axis_size("col")
    own_rows, own_cols = eigvecs.shape
    nb = refl_t.shape[2]
    n_blocks = plan.shape[1]
    pairs = n_col // 2

    def send(x, row_by, col_by):
        to = [
            (r * n_col + c, (r ^ row_by) * n_col + (c ^ col_by[r % 2]))
            for r in range(n_row)
            for c in range(n_col)
        ]
        return lax.ppermute(x, AXES, to)

    wire = pack(refl_v, refl_t)
    got = []
    for step in range(pairs):
        by = (n_col - 1 - 2 * step, n_col - 2 - 2 * step)
        if step == pairs - 1:
            by = (1, 1)
        got.append(send(wire, 0, by))
    parts = {0: eigvecs}
    for step in range(2, n_row, 2):
        parts[step] = send(eigvecs, step, (0, 0))
    swaps = [send(x, 1, (0, 0)) for x in got[:-1]]
    for step in range(0, n_row, 2):
        parts[step + 1] = send(parts[step], 1, (0, 0))
    parts = [parts[step] for step in range(n_row)]
    banks = [wire] + got + swaps

    table = jnp.pad(plan, ((0, 7), (0, nb - n_blocks)), constant_values=offsets[0])
    far = list(range(pairs + 1, n_col))
    near = [slot for slot in range(n_col) if slot not in far]
    vmem = pl.BlockSpec(memory_space=pltpu.VMEM)
    here = pl.BlockSpec(memory_space=pl.ANY)
    pieces = jax.ShapeDtypeStruct((n_col, 8, nb, nb), BF16)
    limit = pltpu.CompilerParams(vmem_limit_bytes=max(12 * 2**20, 8 * n_blocks * 2**17))
    pieces = pl.pallas_call(
        functools.partial(near_kernel, n_col, near),
        out_shape=pieces,
        in_specs=[vmem] * len(near),
        out_specs=vmem,
        compiler_params=limit,
        name="near_entries",
    )(*[banks[slot] for slot in near])
    n_in = 1 + len(far) + n_row
    return pl.pallas_call(
        functools.partial(apply_kernel, n_col, n_row, n_blocks, far),
        out_shape=(jax.ShapeDtypeStruct((own_rows, own_cols), F32), pieces),
        in_specs=[here] + [vmem] * (len(far) + n_row + 1),
        out_specs=(here, vmem),
        scratch_shapes=[
            pltpu.VMEM((n_row * own_rows + 3 * nb, own_cols), F32),
            pltpu.VMEM((n_blocks + 4, 2, nb, own_cols), BF16),
            pltpu.SMEM((8, nb), jnp.int32),
            pltpu.SemaphoreType.DMA((1 + own_rows // nb,)),
        ],
        input_output_aliases={n_in: 1},
        compiler_params=limit,
        name="apply_blocks",
    )(table, *[banks[slot] for slot in far], *parts, pieces)[0]


def solution(mesh):
    in_specs = (P("row", "col"), P(), P(), P("col", None, None), P("col", None, None))
    return jax.shard_map(
        on_device, mesh=mesh, in_specs=in_specs, out_specs=P("row", "col"), check_vma=False
    )
```

```python
import functools

import jax
import jax.numpy as jnp
from jax import lax
from jax.experimental import pallas as pl
from jax.experimental.pallas import tpu as pltpu
from jax.sharding import PartitionSpec as P


AXES = ("row", "col")
F32, BF16 = jnp.float32, jnp.bfloat16


def iotas(rows, cols):
    return lax.broadcasted_iota(jnp.int32, (rows, cols), 0), lax.broadcasted_iota(jnp.int32, (rows, cols), 1)


def pack_kernel(both_any, wire_ref, both_ref, sem):
    nb = wire_ref.shape[1]
    half, quarter = nb // 2, nb // 4
    copy = pltpu.make_async_copy(both_any.at[:, 0, :], both_ref.at[0 : 3 * nb - 1], sem)
    copy.start()
    copy.wait()
    row, col = iotas(nb, nb)
    factor = both_ref[0:nb, :]
    low = both_ref[nb : 2 * nb, :]
    up = pltpu.roll(both_ref[2 * nb - 1 : 3 * nb - 1, :], nb - 1, axis=0)
    wire_ref[0:nb, :] = jnp.where(row > col, low, jnp.where(row < col, up, factor))
    turned = jnp.transpose(jnp.concatenate([factor[half:, :], factor[:half, :]], axis=0))[half:, :]
    row, col = iotas(half, nb)
    square = jnp.where(row < col, factor[:half, :], turned)
    _, col = iotas(quarter, nb)
    wire_ref[nb:, :] = jnp.where(col < half, square[:quarter], pltpu.roll(square[quarter:], half, axis=1))


def pack(vectors, factor):
    nb = factor.shape[2]
    both = jnp.concatenate([factor.reshape(nb, 1, nb), jnp.transpose(vectors, (1, 0, 2))], axis=0)
    return pl.pallas_call(
        pack_kernel,
        out_shape=jax.ShapeDtypeStruct((nb + nb // 4, nb), F32),
        in_specs=[pl.BlockSpec(memory_space=pl.ANY)],
        out_specs=pl.BlockSpec(memory_space=pltpu.VMEM),
        scratch_shapes=[pltpu.VMEM((3 * nb, nb), F32), pltpu.SemaphoreType.DMA],
        compiler_params=pltpu.CompilerParams(vmem_limit_bytes=4 * 2**20),
        name="pack",
    )(both)


def split(x):
    high = x.astype(BF16)
    return high, (x - high.astype(F32)).astype(BF16)


def dot(a, b):
    return jnp.dot(a, b, preferred_element_type=F32)


def dot3(a, b):
    return dot(a[0], b[0]) + (dot(a[1], b[0]) + dot(a[0], b[1]))


def twice(pair):
    return [jnp.concatenate([x, x], axis=0) for x in pair]


def unpack_into(pieces_ref, banks, distances):
    for i in range(0, len(banks), 8):
        unpack_together(pieces_ref, banks[i : i + 8], distances[i : i + 8])


def unpack_together(pieces_ref, banks, distances):
    nb = banks[0].shape[1]
    half = nb // 2
    row, col = iotas(nb, nb)
    row_h, col_h = iotas(half, nb)
    unit = (row == col).astype(F32)
    odd = lax.rem(lax.axis_index("row"), 2)
    my_col = lax.axis_index("col")
    entries = [jnp.bitwise_xor(my_col, even_by + odd * (odd_by - even_by)) for even_by, odd_by in distances]

    across, whole, first, last = [], [], [], []
    for bank, entry in zip(banks, entries):
        square, tail = bank[0:nb, :], bank[nb:, :]
        low = split(jnp.where(row > col, square, unit))
        up = split(jnp.where(row < col, square, 0.0))
        for i in range(2):
            pieces_ref[entry, i] = low[i]
            pieces_ref[entry, 2 + i] = up[i]
        whole.append([jnp.concatenate([low[i], up[i]], axis=0) for i in range(2)])
        turned = jnp.transpose(square)
        turned = [jnp.where(row < col, turned, unit), jnp.where(row > col, turned, 0.0)]
        across.append(jnp.concatenate(turned, axis=1))
        tail = jnp.concatenate([tail, pltpu.roll(tail, half, axis=1)], axis=0)
        below = jnp.where(row_h > col_h, tail, 0.0)
        below = jnp.transpose(jnp.concatenate([jnp.zeros_like(below), below], axis=0))[:half, :]
        above = jnp.where((row_h < col_h) & (col_h < half), tail, 0.0)
        first.append(split(jnp.where(row_h == col_h, square[:half], above)))
        last.append(split(jnp.where(row_h + half == col_h, square[half:], below)))
    split_across = [split(x) for x in across]
    lead_last = [split(dot3(x, y)) for x, y in zip(last, split_across)]
    beside = [dot3([x[:half] for x in y], z) for y, z in zip(split_across, whole)]
    beside = [split(jnp.where(col_h < half, 0.0, x)) for x in beside]
    rest = [split(x[:half] - dot3(y, twice(z))) for x, y, z in zip(across, beside, lead_last)]
    lead_first = [split(dot3(x, twice(y))) for x, y in zip(first, rest)]
    for entry, top, bottom in zip(entries, lead_first, lead_last):
        for i in range(2):
            for part in range(2):
                lanes = slice(part * nb, (part + 1) * nb)
                pieces_ref[entry, 4 + 2 * part + i, 0:half] = top[i][:, lanes]
                pieces_ref[entry, 4 + 2 * part + i, half:nb] = bottom[i][:, lanes]


def unpack_kernel(distances, *refs):
    unpack_into(refs[-1], refs[: len(distances)], distances)


def apply_kernel(distances, n_row, n_blocks, *refs):
    table_any, refs = refs[0], refs[1:]
    banks, refs = refs[: len(distances)], refs[len(distances) :]
    parts, refs = refs[:n_row], refs[n_row:]
    _, out_any, pieces_ref, rows_ref, solved_ref, plan_ref, sems = refs
    nb = pieces_ref.shape[2]
    own_rows, own_cols = parts[0].shape
    my_row = lax.axis_index("row")
    table = pltpu.make_async_copy(table_any, plan_ref, sems.at[0])
    table.start()

    for step in range(n_row):
        start = pl.multiple_of(jnp.bitwise_xor(my_row, step) * own_rows + nb, nb)
        rows_ref[pl.ds(start, own_rows), :] = parts[step][...]
    unpack_into(pieces_ref, banks, distances)

    zero = jnp.zeros((nb, own_cols), BF16)
    for index in (0, 1, n_blocks + 2, n_blocks + 3):
        for i in range(2):
            solved_ref[index, i] = zero
    table.wait()
    first = plan_ref[0, n_blocks]

    def low_of(entry):
        return pieces_ref[entry, 0], pieces_ref[entry, 1]

    def up_of(entry):
        return pieces_ref[entry, 2], pieces_ref[entry, 3]

    def block(index):
        entry = plan_ref[0, index]
        before = plan_ref[0, jnp.maximum(index - 1, 0)]
        window = split(rows_ref[pl.ds(first + (index + 1) * nb, 2 * nb), :])
        lead_low = pieces_ref[entry, 4], pieces_ref[entry, 5]
        lead = [jnp.concatenate([lead_low[i], pieces_ref[entry, 6 + i]], axis=1) for i in range(2)]
        free = dot3(lead, window)
        link = split(dot3(lead_low, up_of(before)))
        return free, link

    def store(index, value):
        value = split(value)
        for i in range(2):
            solved_ref[index + 2, i] = value[i]
        return value

    def solved_of(index):
        return solved_ref[index + 2, 0], solved_ref[index + 2, 1]

    if n_blocks <= 8:
        work = [block(index) for index in range(n_blocks)]
        last = store(0, work[0][0])
        odd = last
        for index in range(1, n_blocks, 2):
            before, (free, link) = work[index - 1], work[index]
            joined = free - dot3(link, last if index == 1 else split(before[0]))
            if index == 1:
                odd = store(index, joined)
                continue
            both = split(dot3(link, before[1]))
            store(index - 1, before[0] - dot3(before[1], odd))
            odd = store(index, joined + dot3(both, odd))
        if n_blocks % 2 and n_blocks > 1:
            free, link = work[-1]
            store(n_blocks - 1, free - dot3(link, odd))
    else:
        store(0, block(0)[0])

        def step(index, carry):
            free, link = block(index)
            store(index, free - dot3(link, solved_of(index - 1)))
            return carry

        lax.fori_loop(1, n_blocks, step, 0)

    mine = my_row * own_rows
    tile = lax.div(mine - first + nb, nb) - 1
    copies = []
    for k in range(own_rows // nb + 1):
        t = jnp.minimum(tile + k, n_blocks + 1)
        low_entry = plan_ref[0, jnp.clip(t, 0, n_blocks - 1)]
        up_entry = plan_ref[0, jnp.clip(t - 1, 0, n_blocks - 1)]
        window = pl.ds(first + (t + 1) * nb, nb)
        moved = dot3(up_of(up_entry), solved_of(t - 1)) + dot3(low_of(low_entry), solved_of(t))
        rows_ref[window, :] = rows_ref[window, :] - moved
        if k > 0:
            source = pl.ds(pl.multiple_of(mine + k * nb, nb), nb)
            copy = pltpu.make_async_copy(
                rows_ref.at[source, :], out_any.at[pl.ds((k - 1) * nb, nb), :], sems.at[k]
            )
            copy.start()
            copies.append(copy)
    for copy in copies:
        copy.wait()


def rounds_of(n_col):
    far = list(zip(range(n_col // 2, n_col, 2), range(n_col - 1, n_col // 2, -2)))
    return far[:0:-1] + [(by, by + 1) for by in range(2, n_col // 2, 2)] + far[:1]


def on_device(eigvecs, offsets, plan, refl_v, refl_t):
    n_row, n_col = lax.axis_size("row"), lax.axis_size("col")
    own_rows, own_cols = eigvecs.shape
    nb = refl_t.shape[2]
    n_blocks = plan.shape[1]

    def send(x, row_by, col_by):
        to = [
            (r * n_col + c, (r ^ row_by) * n_col + (c ^ col_by[r % 2]))
            for r in range(n_row)
            for c in range(n_col)
        ]
        return lax.ppermute(x, AXES, to)

    wire = pack(refl_v, refl_t)
    got = [(send(wire, 0, by), by) for by in rounds_of(n_col)]
    near = (send(wire, 0, (1, 1)), (1, 1))
    parts = {0: eigvecs}
    for step in range(2, n_row, 2):
        parts[step] = send(eigvecs, step, (0, 0))
    swaps = [(send(x, 1, (0, 0)), by[::-1]) for x, by in got]
    for step in range(0, n_row, 2):
        parts[step + 1] = send(parts[step], 1, (0, 0))
    parts = [parts[step] for step in range(n_row)]

    table = jnp.pad(plan, ((0, 7), (0, nb - n_blocks)), constant_values=offsets[0])
    vmem = pl.BlockSpec(memory_space=pltpu.VMEM)
    here = pl.BlockSpec(memory_space=pl.ANY)
    shape = jax.ShapeDtypeStruct((n_col, 8, nb, nb), BF16)
    limit = pltpu.CompilerParams(vmem_limit_bytes=max(12 * 2**20, 8 * n_blocks * 2**17))
    early, late = [(wire, (0, 0)), near] + got + swaps[:-1], swaps[-1:]
    pieces = pl.pallas_call(
        functools.partial(unpack_kernel, [by for _, by in early]),
        out_shape=shape,
        in_specs=[vmem] * len(early),
        out_specs=vmem,
        compiler_params=limit,
        name="unpack_early",
    )(*[x for x, _ in early])
    n_in = 1 + len(late) + n_row
    return pl.pallas_call(
        functools.partial(apply_kernel, [by for _, by in late], n_row, n_blocks),
        out_shape=(jax.ShapeDtypeStruct((own_rows, own_cols), F32), shape),
        in_specs=[here] + [vmem] * (len(late) + n_row + 1),
        out_specs=(here, vmem),
        scratch_shapes=[
            pltpu.VMEM((n_row * own_rows + 3 * nb, own_cols), F32),
            pltpu.VMEM((n_blocks + 4, 2, nb, own_cols), BF16),
            pltpu.SMEM((8, nb), jnp.int32),
            pltpu.SemaphoreType.DMA((1 + own_rows // nb,)),
        ],
        input_output_aliases={n_in: 1},
        compiler_params=limit,
        name="apply_blocks",
    )(table, *[x for x, _ in late], *parts, pieces)[0]


def solution(mesh):
    in_specs = (P("row", "col"), P(), P(), P("col", None, None), P("col", None, None))
    return jax.shard_map(
        on_device, mesh=mesh, in_specs=in_specs, out_specs=P("row", "col"), check_vma=False
    )
```

```python
import functools

import jax
import jax.numpy as jnp
from jax import lax
from jax.experimental import pallas as pl
from jax.experimental.pallas import tpu as pltpu
from jax.sharding import PartitionSpec as P


AXES = ("row", "col")
F32, BF16 = jnp.float32, jnp.bfloat16


def iotas(rows, cols):
    return lax.broadcasted_iota(jnp.int32, (rows, cols), 0), lax.broadcasted_iota(jnp.int32, (rows, cols), 1)


def pack_kernel(both_any, wire_ref, both_ref, sem):
    nb = wire_ref.shape[1]
    half, quarter = nb // 2, nb // 4
    copy = pltpu.make_async_copy(both_any.at[:, 0, :], both_ref.at[0 : 3 * nb - 1], sem)
    copy.start()
    copy.wait()
    row, col = iotas(nb, nb)
    factor = both_ref[0:nb, :]
    low = both_ref[nb : 2 * nb, :]
    up = pltpu.roll(both_ref[2 * nb - 1 : 3 * nb - 1, :], nb - 1, axis=0)
    wire_ref[0:nb, :] = jnp.where(row > col, low, jnp.where(row < col, up, factor))
    turned = jnp.transpose(jnp.concatenate([factor[half:, :], factor[:half, :]], axis=0))[half:, :]
    row, col = iotas(half, nb)
    square = jnp.where(row < col, factor[:half, :], turned)
    _, col = iotas(quarter, nb)
    wire_ref[nb:, :] = jnp.where(col < half, square[:quarter], pltpu.roll(square[quarter:], half, axis=1))


def pack(vectors, factor):
    nb = factor.shape[2]
    both = jnp.concatenate([factor.reshape(nb, 1, nb), jnp.transpose(vectors, (1, 0, 2))], axis=0)
    return pl.pallas_call(
        pack_kernel,
        out_shape=jax.ShapeDtypeStruct((nb + nb // 4, nb), F32),
        in_specs=[pl.BlockSpec(memory_space=pl.ANY)],
        out_specs=pl.BlockSpec(memory_space=pltpu.VMEM),
        scratch_shapes=[pltpu.VMEM((3 * nb, nb), F32), pltpu.SemaphoreType.DMA],
        compiler_params=pltpu.CompilerParams(vmem_limit_bytes=4 * 2**20),
        name="pack",
    )(both)


def split(x):
    high = x.astype(BF16)
    return high, (x - high.astype(F32)).astype(BF16)


def dot(a, b):
    return jnp.dot(a, b, preferred_element_type=F32)


def dot3(a, b):
    n = b[0].shape[1]
    both = dot(a[0], jnp.concatenate(b, axis=1))
    return both[:, :n] + (both[:, n:] + dot(a[1], b[0]))


def twice(pair):
    return [jnp.concatenate([x, x], axis=0) for x in pair]


def unpack_into(pieces_ref, banks, distances):
    for i in range(0, len(banks), 8):
        unpack_together(pieces_ref, banks[i : i + 8], distances[i : i + 8])


def unpack_together(pieces_ref, banks, distances):
    nb = banks[0].shape[1]
    half = nb // 2
    row, col = iotas(nb, nb)
    row_h, col_h = iotas(half, nb)
    unit = (row == col).astype(F32)
    odd = lax.rem(lax.axis_index("row"), 2)
    my_col = lax.axis_index("col")
    entries = [jnp.bitwise_xor(my_col, even_by + odd * (odd_by - even_by)) for even_by, odd_by in distances]

    across, whole, first, last = [], [], [], []
    for bank, entry in zip(banks, entries):
        square, tail = bank[0:nb, :], bank[nb:, :]
        low = split(jnp.where(row > col, square, unit))
        up = split(jnp.where(row < col, square, 0.0))
        for i in range(2):
            pieces_ref[entry, i] = low[i]
            pieces_ref[entry, 2 + i] = up[i]
        whole.append([jnp.concatenate([low[i], up[i]], axis=0) for i in range(2)])
        turned = jnp.transpose(square)
        turned = [jnp.where(row < col, turned, unit), jnp.where(row > col, turned, 0.0)]
        across.append(jnp.concatenate(turned, axis=1))
        tail = jnp.concatenate([tail, pltpu.roll(tail, half, axis=1)], axis=0)
        below = jnp.where(row_h > col_h, tail, 0.0)
        below = jnp.transpose(jnp.concatenate([jnp.zeros_like(below), below], axis=0))[:half, :]
        above = jnp.where((row_h < col_h) & (col_h < half), tail, 0.0)
        first.append(split(jnp.where(row_h == col_h, square[:half], above)))
        last.append(split(jnp.where(row_h + half == col_h, square[half:], below)))
    split_across = [split(x) for x in across]
    lead_last = [split(dot3(x, y)) for x, y in zip(last, split_across)]
    beside = [dot3([x[:half] for x in y], z) for y, z in zip(split_across, whole)]
    beside = [split(jnp.where(col_h < half, 0.0, x)) for x in beside]
    rest = [split(x[:half] - dot3(y, twice(z))) for x, y, z in zip(across, beside, lead_last)]
    lead_first = [split(dot3(x, twice(y))) for x, y in zip(first, rest)]
    for entry, top, bottom in zip(entries, lead_first, lead_last):
        for i in range(2):
            for part in range(2):
                lanes = slice(part * nb, (part + 1) * nb)
                pieces_ref[entry, 4 + 2 * part + i, 0:half] = top[i][:, lanes]
                pieces_ref[entry, 4 + 2 * part + i, half:nb] = bottom[i][:, lanes]


def unpack_kernel(distances, *refs):
    unpack_into(refs[-1], refs[: len(distances)], distances)


def apply_kernel(distances, n_row, n_blocks, *refs):
    table_any, refs = refs[0], refs[1:]
    banks, refs = refs[: len(distances)], refs[len(distances) :]
    parts, refs = refs[:n_row], refs[n_row:]
    _, out_any, pieces_ref, rows_ref, solved_ref, plan_ref, sems = refs
    nb = pieces_ref.shape[2]
    own_rows, own_cols = parts[0].shape
    my_row = lax.axis_index("row")
    table = pltpu.make_async_copy(table_any, plan_ref, sems.at[0])
    table.start()

    for step in range(n_row):
        start = pl.multiple_of(jnp.bitwise_xor(my_row, step) * own_rows + nb, nb)
        rows_ref[pl.ds(start, own_rows), :] = parts[step][...]
    unpack_into(pieces_ref, banks, distances)

    zero = jnp.zeros((nb, own_cols), BF16)
    for index in (0, 1, n_blocks + 2, n_blocks + 3):
        for i in range(2):
            solved_ref[index, i] = zero
    table.wait()
    first = plan_ref[0, n_blocks]

    def low_of(entry):
        return pieces_ref[entry, 0], pieces_ref[entry, 1]

    def up_of(entry):
        return pieces_ref[entry, 2], pieces_ref[entry, 3]

    def block(index):
        entry = plan_ref[0, index]
        before = plan_ref[0, jnp.maximum(index - 1, 0)]
        window = split(rows_ref[pl.ds(first + (index + 1) * nb, 2 * nb), :])
        lead_low = pieces_ref[entry, 4], pieces_ref[entry, 5]
        lead = [jnp.concatenate([lead_low[i], pieces_ref[entry, 6 + i]], axis=1) for i in range(2)]
        free = dot3(lead, window)
        link = split(dot3(lead_low, up_of(before)))
        return free, link

    def store(index, value):
        value = split(value)
        for i in range(2):
            solved_ref[index + 2, i] = value[i]
        return value

    def solved_of(index):
        return solved_ref[index + 2, 0], solved_ref[index + 2, 1]

    if n_blocks <= 8:
        work = [block(index) for index in range(n_blocks)]
        last = store(0, work[0][0])
        odd = last
        for index in range(1, n_blocks, 2):
            before, (free, link) = work[index - 1], work[index]
            joined = free - dot3(link, last if index == 1 else split(before[0]))
            if index == 1:
                odd = store(index, joined)
                continue
            both = split(dot3(link, before[1]))
            store(index - 1, before[0] - dot3(before[1], odd))
            odd = store(index, joined + dot3(both, odd))
        if n_blocks % 2 and n_blocks > 1:
            free, link = work[-1]
            store(n_blocks - 1, free - dot3(link, odd))
    else:
        store(0, block(0)[0])

        def step(index, carry):
            free, link = block(index)
            store(index, free - dot3(link, solved_of(index - 1)))
            return carry

        lax.fori_loop(1, n_blocks, step, 0)

    mine = my_row * own_rows
    tile = lax.div(mine - first + nb, nb) - 1
    windows, values = [], []
    for k in range(own_rows // nb + 1):
        t = jnp.minimum(tile + k, n_blocks + 1)
        low = low_of(plan_ref[0, jnp.clip(t, 0, n_blocks - 1)])
        up = up_of(plan_ref[0, jnp.clip(t - 1, 0, n_blocks - 1)])
        both = [jnp.concatenate([up[i], low[i]], axis=1) for i in range(2)]
        solved = [jnp.concatenate([solved_of(t - 1)[i], solved_of(t)[i]], axis=0) for i in range(2)]
        windows.append(pl.ds(first + (t + 1) * nb, nb))
        values.append(rows_ref[windows[-1], :] - dot3(both, solved))
    copies = []
    for k, (window, value) in enumerate(zip(windows, values)):
        rows_ref[window, :] = value
        if k > 0:
            source = pl.ds(pl.multiple_of(mine + k * nb, nb), nb)
            copy = pltpu.make_async_copy(
                rows_ref.at[source, :], out_any.at[pl.ds((k - 1) * nb, nb), :], sems.at[k]
            )
            copy.start()
            copies.append(copy)
    for copy in copies:
        copy.wait()


def rounds_of(n_col):
    far = list(zip(range(n_col // 2, n_col, 2), range(n_col - 1, n_col // 2, -2)))
    return far[:0:-1] + [(by, by + 1) for by in range(2, n_col // 2, 2)] + far[:1]


def on_device(eigvecs, offsets, plan, refl_v, refl_t):
    n_row, n_col = lax.axis_size("row"), lax.axis_size("col")
    own_rows, own_cols = eigvecs.shape
    nb = refl_t.shape[2]
    n_blocks = plan.shape[1]

    def send(x, row_by, col_by):
        to = [
            (r * n_col + c, (r ^ row_by) * n_col + (c ^ col_by[r % 2]))
            for r in range(n_row)
            for c in range(n_col)
        ]
        return lax.ppermute(x, AXES, to)

    wire = pack(refl_v, refl_t)
    got = [(send(wire, 0, by), by) for by in rounds_of(n_col)]
    near = (send(wire, 0, (1, 1)), (1, 1))
    parts = {0: eigvecs}
    for step in range(2, n_row, 2):
        parts[step] = send(eigvecs, step, (0, 0))
    swaps = [(send(x, 1, (0, 0)), by[::-1]) for x, by in got]
    for step in range(0, n_row, 2):
        parts[step + 1] = send(parts[step], 1, (0, 0))
    parts = [parts[step] for step in range(n_row)]

    table = jnp.pad(plan, ((0, 7), (0, nb - n_blocks)), constant_values=offsets[0])
    vmem = pl.BlockSpec(memory_space=pltpu.VMEM)
    here = pl.BlockSpec(memory_space=pl.ANY)
    shape = jax.ShapeDtypeStruct((n_col, 8, nb, nb), BF16)
    limit = pltpu.CompilerParams(vmem_limit_bytes=max(12 * 2**20, 8 * n_blocks * 2**17))
    early, late = [(wire, (0, 0)), near] + got + swaps[:-1], swaps[-1:]
    pieces = pl.pallas_call(
        functools.partial(unpack_kernel, [by for _, by in early]),
        out_shape=shape,
        in_specs=[vmem] * len(early),
        out_specs=vmem,
        compiler_params=limit,
        name="unpack_early",
    )(*[x for x, _ in early])
    n_in = 1 + len(late) + n_row
    return pl.pallas_call(
        functools.partial(apply_kernel, [by for _, by in late], n_row, n_blocks),
        out_shape=(jax.ShapeDtypeStruct((own_rows, own_cols), F32), shape),
        in_specs=[here] + [vmem] * (len(late) + n_row + 1),
        out_specs=(here, vmem),
        scratch_shapes=[
            pltpu.VMEM((n_row * own_rows + 3 * nb, own_cols), F32),
            pltpu.VMEM((n_blocks + 4, 2, nb, own_cols), BF16),
            pltpu.SMEM((8, nb), jnp.int32),
            pltpu.SemaphoreType.DMA((1 + own_rows // nb,)),
        ],
        input_output_aliases={n_in: 1},
        compiler_params=limit,
        name="apply_blocks",
    )(table, *[x for x, _ in late], *parts, pieces)[0]


def solution(mesh):
    in_specs = (P("row", "col"), P(), P(), P("col", None, None), P("col", None, None))
    return jax.shard_map(
        on_device, mesh=mesh, in_specs=in_specs, out_specs=P("row", "col"), check_vma=False
    )
```

```python
import functools

import jax
import jax.numpy as jnp
from jax import lax
from jax.experimental import pallas as pl
from jax.experimental.pallas import tpu as pltpu
from jax.sharding import PartitionSpec as P


AXES = ("row", "col")
F32, BF16 = jnp.float32, jnp.bfloat16


def iotas(rows, cols):
    return lax.broadcasted_iota(jnp.int32, (rows, cols), 0), lax.broadcasted_iota(jnp.int32, (rows, cols), 1)


def pack_kernel(both_ref, wire_ref):
    nb = wire_ref.shape[1]
    half, quarter = nb // 2, nb // 4
    row, col = iotas(nb, nb)
    factor = both_ref[0:nb, 0, :]
    low = both_ref[nb : 2 * nb, 0, :]
    up = pltpu.roll(both_ref[2 * nb - 1 : 3 * nb - 1, 0, :], nb - 1, axis=0)
    wire_ref[0:nb, :] = jnp.where(row > col, low, jnp.where(row < col, up, factor))
    turned = jnp.transpose(jnp.concatenate([factor[half:, :], factor[:half, :]], axis=0))[half:, :]
    row, col = iotas(half, nb)
    square = jnp.where(row < col, factor[:half, :], turned)
    _, col = iotas(quarter, nb)
    wire_ref[nb:, :] = jnp.where(col < half, square[:quarter], pltpu.roll(square[quarter:], half, axis=1))


def pack(vectors, factor):
    nb = factor.shape[2]
    both = jnp.concatenate([factor.reshape(nb, 1, nb), jnp.transpose(vectors, (1, 0, 2))], axis=0)
    return pl.pallas_call(
        pack_kernel,
        out_shape=jax.ShapeDtypeStruct((nb + nb // 4, nb), F32),
        compiler_params=pltpu.CompilerParams(vmem_limit_bytes=4 * 2**20),
        name="pack",
    )(both)


def split(x):
    high = x.astype(BF16)
    return high, (x - high.astype(F32)).astype(BF16)


def dot(a, b):
    return jnp.dot(a, b, preferred_element_type=F32)


def dot3(a, b):
    n = b[0].shape[1]
    both = dot(a[0], jnp.concatenate(b, axis=1))
    return both[:, :n] + (both[:, n:] + dot(a[1], b[0]))


def twice(pair):
    return [jnp.concatenate([x, x], axis=0) for x in pair]


def unpack_into(pieces_ref, banks, distances):
    for i in range(0, len(banks), 8):
        unpack_together(pieces_ref, banks[i : i + 8], distances[i : i + 8])


def unpack_together(pieces_ref, banks, distances):
    nb = banks[0].shape[1]
    half = nb // 2
    row, col = iotas(nb, nb)
    row_h, col_h = iotas(half, nb)
    unit = (row == col).astype(F32)
    odd = lax.rem(lax.axis_index("row"), 2)
    my_col = lax.axis_index("col")
    entries = [jnp.bitwise_xor(my_col, even_by + odd * (odd_by - even_by)) for even_by, odd_by in distances]

    across, whole, first, last = [], [], [], []
    for bank, entry in zip(banks, entries):
        square, tail = bank[0:nb, :], bank[nb:, :]
        low = split(jnp.where(row > col, square, unit))
        up = split(jnp.where(row < col, square, 0.0))
        for i in range(2):
            pieces_ref[entry, i] = low[i]
            pieces_ref[entry, 2 + i] = up[i]
        whole.append([jnp.concatenate([low[i], up[i]], axis=0) for i in range(2)])
        turned = jnp.transpose(square)
        turned = [jnp.where(row < col, turned, unit), jnp.where(row > col, turned, 0.0)]
        across.append(jnp.concatenate(turned, axis=1))
        tail = jnp.concatenate([tail, pltpu.roll(tail, half, axis=1)], axis=0)
        below = jnp.where(row_h > col_h, tail, 0.0)
        below = jnp.transpose(jnp.concatenate([jnp.zeros_like(below), below], axis=0))[:half, :]
        above = jnp.where((row_h < col_h) & (col_h < half), tail, 0.0)
        first.append(split(jnp.where(row_h == col_h, square[:half], above)))
        last.append(split(jnp.where(row_h + half == col_h, square[half:], below)))
    split_across = [split(x) for x in across]
    lead_last = [split(dot3(x, y)) for x, y in zip(last, split_across)]
    beside = [dot3([x[:half] for x in y], z) for y, z in zip(split_across, whole)]
    beside = [split(jnp.where(col_h < half, 0.0, x)) for x in beside]
    rest = [split(x[:half] - dot3(y, twice(z))) for x, y, z in zip(across, beside, lead_last)]
    lead_first = [split(dot3(x, twice(y))) for x, y in zip(first, rest)]
    for entry, top, bottom in zip(entries, lead_first, lead_last):
        for i in range(2):
            for part in range(2):
                lanes = slice(part * nb, (part + 1) * nb)
                pieces_ref[entry, 4 + 2 * part + i, 0:half] = top[i][:, lanes]
                pieces_ref[entry, 4 + 2 * part + i, half:nb] = bottom[i][:, lanes]


def unpack_kernel(distances, *refs):
    unpack_into(refs[-1], refs[: len(distances)], distances)


def apply_kernel(distances, n_row, n_blocks, *refs):
    table_any, refs = refs[0], refs[1:]
    banks, refs = refs[: len(distances)], refs[len(distances) :]
    parts, refs = refs[:n_row], refs[n_row:]
    _, out_any, pieces_ref, rows_ref, solved_ref, plan_ref, sems = refs
    nb = pieces_ref.shape[2]
    own_rows, own_cols = parts[0].shape
    my_row = lax.axis_index("row")
    table = pltpu.make_async_copy(table_any, plan_ref, sems.at[0])
    table.start()

    for step in range(n_row):
        start = pl.multiple_of(jnp.bitwise_xor(my_row, step) * own_rows + nb, nb)
        rows_ref[pl.ds(start, own_rows), :] = parts[step][...]
    unpack_into(pieces_ref, banks, distances)

    zero = jnp.zeros((nb, own_cols), BF16)
    for index in (0, 1, n_blocks + 2, n_blocks + 3):
        for i in range(2):
            solved_ref[index, i] = zero
    table.wait()
    first = plan_ref[0, n_blocks]

    def low_of(entry):
        return pieces_ref[entry, 0], pieces_ref[entry, 1]

    def up_of(entry):
        return pieces_ref[entry, 2], pieces_ref[entry, 3]

    def block(index):
        entry = plan_ref[0, index]
        before = plan_ref[0, jnp.maximum(index - 1, 0)]
        window = split(rows_ref[pl.ds(first + (index + 1) * nb, 2 * nb), :])
        lead_low = pieces_ref[entry, 4], pieces_ref[entry, 5]
        lead = [jnp.concatenate([lead_low[i], pieces_ref[entry, 6 + i]], axis=1) for i in range(2)]
        free = dot3(lead, window)
        link = split(dot3(lead_low, up_of(before)))
        return free, link

    def store(index, value):
        value = split(value)
        for i in range(2):
            solved_ref[index + 2, i] = value[i]
        return value

    def solved_of(index):
        return solved_ref[index + 2, 0], solved_ref[index + 2, 1]

    if n_blocks <= 8:
        work = [block(index) for index in range(n_blocks)]
        last = store(0, work[0][0])
        odd = last
        for index in range(1, n_blocks, 2):
            before, (free, link) = work[index - 1], work[index]
            joined = free - dot3(link, last if index == 1 else split(before[0]))
            if index == 1:
                odd = store(index, joined)
                continue
            both = split(dot3(link, before[1]))
            store(index - 1, before[0] - dot3(before[1], odd))
            odd = store(index, joined + dot3(both, odd))
        if n_blocks % 2 and n_blocks > 1:
            free, link = work[-1]
            store(n_blocks - 1, free - dot3(link, odd))
    else:
        store(0, block(0)[0])

        def step(index, carry):
            free, link = block(index)
            store(index, free - dot3(link, solved_of(index - 1)))
            return carry

        lax.fori_loop(1, n_blocks, step, 0)

    mine = my_row * own_rows
    tile = lax.div(mine - first + nb, nb) - 1
    windows, values = [], []
    for k in range(own_rows // nb + 1):
        t = jnp.minimum(tile + k, n_blocks + 1)
        low = low_of(plan_ref[0, jnp.clip(t, 0, n_blocks - 1)])
        up = up_of(plan_ref[0, jnp.clip(t - 1, 0, n_blocks - 1)])
        both = [jnp.concatenate([up[i], low[i]], axis=1) for i in range(2)]
        solved = [jnp.concatenate([solved_of(t - 1)[i], solved_of(t)[i]], axis=0) for i in range(2)]
        windows.append(pl.ds(first + (t + 1) * nb, nb))
        values.append(rows_ref[windows[-1], :] - dot3(both, solved))
    copies = []
    for k, (window, value) in enumerate(zip(windows, values)):
        rows_ref[window, :] = value
        if k > 0:
            source = pl.ds(pl.multiple_of(mine + k * nb, nb), nb)
            copy = pltpu.make_async_copy(
                rows_ref.at[source, :], out_any.at[pl.ds((k - 1) * nb, nb), :], sems.at[k]
            )
            copy.start()
            copies.append(copy)
    for copy in copies:
        copy.wait()


def rounds_of(n_col):
    far = list(zip(range(n_col // 2, n_col, 2), range(n_col - 1, n_col // 2, -2)))
    return far[:0:-1] + [(by + 1, by) for by in range(2, n_col // 2, 2)] + far[:1]


def on_device(eigvecs, offsets, plan, refl_v, refl_t):
    n_row, n_col = lax.axis_size("row"), lax.axis_size("col")
    own_rows, own_cols = eigvecs.shape
    nb = refl_t.shape[2]
    n_blocks = plan.shape[1]

    def send(x, row_by, col_by):
        to = [
            (r * n_col + c, (r ^ row_by) * n_col + (c ^ col_by[r % 2]))
            for r in range(n_row)
            for c in range(n_col)
        ]
        return lax.ppermute(x, AXES, to)

    wire = pack(refl_v, refl_t)
    got = [(send(wire, 0, by), by) for by in rounds_of(n_col)]
    near = (send(wire, 0, (1, 1)), (1, 1))
    parts = {0: eigvecs}
    for step in range(2, n_row, 2):
        parts[step] = send(eigvecs, step, (0, 0))
    swaps = [(send(x, 1, (0, 0)), by[::-1]) for x, by in got]
    for step in range(0, n_row, 2):
        parts[step + 1] = send(parts[step], 1, (0, 0))
    parts = [parts[step] for step in range(n_row)]

    table = jnp.pad(plan, ((0, 7), (0, nb - n_blocks)), constant_values=offsets[0])
    vmem = pl.BlockSpec(memory_space=pltpu.VMEM)
    here = pl.BlockSpec(memory_space=pl.ANY)
    shape = jax.ShapeDtypeStruct((n_col, 8, nb, nb), BF16)
    limit = pltpu.CompilerParams(vmem_limit_bytes=max(12 * 2**20, 8 * n_blocks * 2**17))
    early, late = [(wire, (0, 0)), near] + got + swaps[:-1], swaps[-1:]
    pieces = pl.pallas_call(
        functools.partial(unpack_kernel, [by for _, by in early]),
        out_shape=shape,
        in_specs=[vmem] * len(early),
        out_specs=vmem,
        compiler_params=limit,
        name="unpack_early",
    )(*[x for x, _ in early])
    n_in = 1 + len(late) + n_row
    return pl.pallas_call(
        functools.partial(apply_kernel, [by for _, by in late], n_row, n_blocks),
        out_shape=(jax.ShapeDtypeStruct((own_rows, own_cols), F32), shape),
        in_specs=[here] + [vmem] * (len(late) + n_row + 1),
        out_specs=(here, vmem),
        scratch_shapes=[
            pltpu.VMEM((n_row * own_rows + 3 * nb, own_cols), F32),
            pltpu.VMEM((n_blocks + 4, 2, nb, own_cols), BF16),
            pltpu.SMEM((8, nb), jnp.int32),
            pltpu.SemaphoreType.DMA((1 + own_rows // nb,)),
        ],
        input_output_aliases={n_in: 1},
        compiler_params=limit,
        name="apply_blocks",
    )(table, *[x for x, _ in late], *parts, pieces)[0]


def solution(mesh):
    in_specs = (P("row", "col"), P(), P(), P("col", None, None), P("col", None, None))
    return jax.shard_map(
        on_device, mesh=mesh, in_specs=in_specs, out_specs=P("row", "col"), check_vma=False
    )
```

```python
import functools

import jax
import jax.numpy as jnp
from jax import lax
from jax.experimental import pallas as pl
from jax.experimental.pallas import tpu as pltpu
from jax.sharding import PartitionSpec as P


AXES = ("row", "col")
F32, BF16 = jnp.float32, jnp.bfloat16


def iotas(rows, cols):
    return lax.broadcasted_iota(jnp.int32, (rows, cols), 0), lax.broadcasted_iota(jnp.int32, (rows, cols), 1)


def pack_kernel(both_ref, wire_ref):
    nb = wire_ref.shape[1]
    half, quarter = nb // 2, nb // 4
    row, col = iotas(nb, nb)
    factor = both_ref[0:nb, 0, :]
    low = both_ref[nb : 2 * nb, 0, :]
    up = pltpu.roll(both_ref[2 * nb - 1 : 3 * nb - 1, 0, :], nb - 1, axis=0)
    wire_ref[0:nb, :] = jnp.where(row > col, low, jnp.where(row < col, up, factor))
    turned = jnp.transpose(jnp.concatenate([factor[half:, :], factor[:half, :]], axis=0))[half:, :]
    row, col = iotas(half, nb)
    square = jnp.where(row < col, factor[:half, :], turned)
    _, col = iotas(quarter, nb)
    wire_ref[nb:, :] = jnp.where(col < half, square[:quarter], pltpu.roll(square[quarter:], half, axis=1))


def pack(vectors, factor):
    nb = factor.shape[2]
    both = jnp.concatenate([factor.reshape(nb, 1, nb), jnp.transpose(vectors, (1, 0, 2))], axis=0)
    return pl.pallas_call(
        pack_kernel,
        out_shape=jax.ShapeDtypeStruct((nb + nb // 4, nb), F32),
        compiler_params=pltpu.CompilerParams(vmem_limit_bytes=4 * 2**20),
        name="pack",
    )(both)


def split(x):
    high = x.astype(BF16)
    return high, (x - high.astype(F32)).astype(BF16)


def dot(a, b):
    return jnp.dot(a, b, preferred_element_type=F32)


def dot3(a, b):
    n = b[0].shape[1]
    both = dot(a[0], jnp.concatenate(b, axis=1))
    return both[:, :n] + (both[:, n:] + dot(a[1], b[0]))


def twice(pair):
    return [jnp.concatenate([x, x], axis=0) for x in pair]


def unpack_into(pieces_ref, banks, distances):
    for i in range(0, len(banks), 8):
        unpack_together(pieces_ref, banks[i : i + 8], distances[i : i + 8])


def unpack_together(pieces_ref, banks, distances):
    nb = banks[0].shape[1]
    half = nb // 2
    row, col = iotas(nb, nb)
    row_h, col_h = iotas(half, nb)
    unit = (row == col).astype(F32)
    odd = lax.rem(lax.axis_index("row"), 2)
    my_col = lax.axis_index("col")
    entries = [jnp.bitwise_xor(my_col, even_by + odd * (odd_by - even_by)) for even_by, odd_by in distances]

    across, whole, first, last = [], [], [], []
    for bank, entry in zip(banks, entries):
        square, tail = bank[0:nb, :], bank[nb:, :]
        low = split(jnp.where(row > col, square, unit))
        up = split(jnp.where(row < col, square, 0.0))
        for i in range(2):
            pieces_ref[entry, i] = low[i]
            pieces_ref[entry, 2 + i] = up[i]
        whole.append([jnp.concatenate([low[i], up[i]], axis=0) for i in range(2)])
        turned = jnp.transpose(square)
        turned = [jnp.where(row < col, turned, unit), jnp.where(row > col, turned, 0.0)]
        across.append(jnp.concatenate(turned, axis=1))
        tail = jnp.concatenate([tail, pltpu.roll(tail, half, axis=1)], axis=0)
        below = jnp.where(row_h > col_h, tail, 0.0)
        below = jnp.transpose(jnp.concatenate([jnp.zeros_like(below), below], axis=0))[:half, :]
        above = jnp.where((row_h < col_h) & (col_h < half), tail, 0.0)
        first.append(split(jnp.where(row_h == col_h, square[:half], above)))
        last.append(split(jnp.where(row_h + half == col_h, square[half:], below)))
    split_across = [split(x) for x in across]
    lead_last = [split(dot3(x, y)) for x, y in zip(last, split_across)]
    beside = [dot3([x[:half] for x in y], z) for y, z in zip(split_across, whole)]
    beside = [split(jnp.where(col_h < half, 0.0, x)) for x in beside]
    rest = [split(x[:half] - dot3(y, twice(z))) for x, y, z in zip(across, beside, lead_last)]
    lead_first = [split(dot3(x, twice(y))) for x, y in zip(first, rest)]
    for entry, top, bottom in zip(entries, lead_first, lead_last):
        for i in range(2):
            for part in range(2):
                lanes = slice(part * nb, (part + 1) * nb)
                pieces_ref[entry, 4 + 2 * part + i, 0:half] = top[i][:, lanes]
                pieces_ref[entry, 4 + 2 * part + i, half:nb] = bottom[i][:, lanes]


def unpack_kernel(distances, *refs):
    unpack_into(refs[-1], refs[: len(distances)], distances)


def dot_deep(a, b):
    return jnp.dot(
        jnp.concatenate([a[0], a[1], a[0]], axis=1),
        jnp.concatenate([b[0], b[0], b[1]], axis=0),
        preferred_element_type=F32,
    )


def apply_kernel(distances, n_row, n_blocks, *refs):
    table_any, refs = refs[0], refs[1:]
    banks, refs = refs[: len(distances)], refs[len(distances) :]
    parts, refs = refs[:n_row], refs[n_row:]
    _, out_any, pieces_ref, rows_ref, solved_ref, plan_ref, sems = refs
    nb = pieces_ref.shape[2]
    own_rows, own_cols = parts[0].shape
    my_row = lax.axis_index("row")
    table = pltpu.make_async_copy(table_any, plan_ref, sems.at[0])
    table.start()

    for step in range(n_row):
        start = pl.multiple_of(jnp.bitwise_xor(my_row, step) * own_rows + nb, nb)
        rows_ref[pl.ds(start, own_rows), :] = parts[step][...]
    unpack_into(pieces_ref, banks, distances)

    zero = jnp.zeros((nb, own_cols), BF16)
    for index in (0, 1, n_blocks + 2, n_blocks + 3):
        for i in range(2):
            solved_ref[index, i] = zero
    table.wait()
    first = plan_ref[0, n_blocks]

    def low_of(entry):
        return pieces_ref[entry, 0], pieces_ref[entry, 1]

    def up_of(entry):
        return pieces_ref[entry, 2], pieces_ref[entry, 3]

    def block(index):
        entry = plan_ref[0, index]
        before = plan_ref[0, jnp.maximum(index - 1, 0)]
        window = split(rows_ref[pl.ds(first + (index + 1) * nb, 2 * nb), :])
        lead_low = pieces_ref[entry, 4], pieces_ref[entry, 5]
        lead = [jnp.concatenate([lead_low[i], pieces_ref[entry, 6 + i]], axis=1) for i in range(2)]
        free = dot3(lead, window)
        link = split(dot3(lead_low, up_of(before)))
        return free, link

    def store(index, value):
        value = split(value)
        for i in range(2):
            solved_ref[index + 2, i] = value[i]
        return value

    def solved_of(index):
        return solved_ref[index + 2, 0], solved_ref[index + 2, 1]

    if n_blocks <= 8:
        work = [block(index) for index in range(n_blocks)]
        last = store(0, work[0][0])
        odd = last
        for index in range(1, n_blocks, 2):
            before, (free, link) = work[index - 1], work[index]
            joined = free - dot3(link, last if index == 1 else split(before[0]))
            if index == 1:
                odd = store(index, joined)
                continue
            both = split(dot3(link, before[1]))
            store(index - 1, before[0] - dot_deep(before[1], odd))
            odd = store(index, joined + dot_deep(both, odd))
        if n_blocks % 2 and n_blocks > 1:
            free, link = work[-1]
            store(n_blocks - 1, free - dot3(link, odd))
    else:
        store(0, block(0)[0])

        def step(index, carry):
            free, link = block(index)
            store(index, free - dot3(link, solved_of(index - 1)))
            return carry

        lax.fori_loop(1, n_blocks, step, 0)

    mine = my_row * own_rows
    tile = lax.div(mine - first + nb, nb) - 1
    windows, values = [], []
    for k in range(own_rows // nb + 1):
        t = jnp.minimum(tile + k, n_blocks + 1)
        low = low_of(plan_ref[0, jnp.clip(t, 0, n_blocks - 1)])
        up = up_of(plan_ref[0, jnp.clip(t - 1, 0, n_blocks - 1)])
        both = [jnp.concatenate([up[i], low[i]], axis=1) for i in range(2)]
        solved = [jnp.concatenate([solved_of(t - 1)[i], solved_of(t)[i]], axis=0) for i in range(2)]
        windows.append(pl.ds(first + (t + 1) * nb, nb))
        values.append(rows_ref[windows[-1], :] - dot3(both, solved))
    copies = []
    for k, (window, value) in enumerate(zip(windows, values)):
        rows_ref[window, :] = value
        if k > 0:
            source = pl.ds(pl.multiple_of(mine + k * nb, nb), nb)
            copy = pltpu.make_async_copy(
                rows_ref.at[source, :], out_any.at[pl.ds((k - 1) * nb, nb), :], sems.at[k]
            )
            copy.start()
            copies.append(copy)
    for copy in copies:
        copy.wait()


def rounds_of(n_col):
    far = list(zip(range(n_col // 2, n_col, 2), range(n_col - 1, n_col // 2, -2)))
    return far[:0:-1] + [(by + 1, by) for by in range(2, n_col // 2, 2)] + far[:1]


def on_device(eigvecs, offsets, plan, refl_v, refl_t):
    n_row, n_col = lax.axis_size("row"), lax.axis_size("col")
    own_rows, own_cols = eigvecs.shape
    nb = refl_t.shape[2]
    n_blocks = plan.shape[1]

    def send(x, row_by, col_by):
        to = [
            (r * n_col + c, (r ^ row_by) * n_col + (c ^ col_by[r % 2]))
            for r in range(n_row)
            for c in range(n_col)
        ]
        return lax.ppermute(x, AXES, to)

    wire = pack(refl_v, refl_t)
    got = [(send(wire, 0, by), by) for by in rounds_of(n_col)]
    near = (send(wire, 0, (1, 1)), (1, 1))
    parts = {0: eigvecs}
    for step in range(2, n_row, 2):
        parts[step] = send(eigvecs, step, (0, 0))
    swaps = [(send(x, 1, (0, 0)), by[::-1]) for x, by in got]
    for step in range(0, n_row, 2):
        parts[step + 1] = send(parts[step], 1, (0, 0))
    parts = [parts[step] for step in range(n_row)]

    table = jnp.pad(plan, ((0, 7), (0, nb - n_blocks)), constant_values=offsets[0])
    vmem = pl.BlockSpec(memory_space=pltpu.VMEM)
    here = pl.BlockSpec(memory_space=pl.ANY)
    shape = jax.ShapeDtypeStruct((n_col, 8, nb, nb), BF16)
    limit = pltpu.CompilerParams(vmem_limit_bytes=max(12 * 2**20, 8 * n_blocks * 2**17))
    early, late = [(wire, (0, 0)), near] + got + swaps[:-1], swaps[-1:]
    pieces = pl.pallas_call(
        functools.partial(unpack_kernel, [by for _, by in early]),
        out_shape=shape,
        in_specs=[vmem] * len(early),
        out_specs=vmem,
        compiler_params=limit,
        name="unpack_early",
    )(*[x for x, _ in early])
    n_in = 1 + len(late) + n_row
    return pl.pallas_call(
        functools.partial(apply_kernel, [by for _, by in late], n_row, n_blocks),
        out_shape=(jax.ShapeDtypeStruct((own_rows, own_cols), F32), shape),
        in_specs=[here] + [vmem] * (len(late) + n_row + 1),
        out_specs=(here, vmem),
        scratch_shapes=[
            pltpu.VMEM((n_row * own_rows + 3 * nb, own_cols), F32),
            pltpu.VMEM((n_blocks + 4, 2, nb, own_cols), BF16),
            pltpu.SMEM((8, nb), jnp.int32),
            pltpu.SemaphoreType.DMA((1 + own_rows // nb,)),
        ],
        input_output_aliases={n_in: 1},
        compiler_params=limit,
        name="apply_blocks",
    )(table, *[x for x, _ in late], *parts, pieces)[0]


def solution(mesh):
    in_specs = (P("row", "col"), P(), P(), P("col", None, None), P("col", None, None))
    return jax.shard_map(
        on_device, mesh=mesh, in_specs=in_specs, out_specs=P("row", "col"), check_vma=False
    )
```
